32 devices in a mesh: space: 16 (over z, y, core), harm: 2 (over x).
Axes of the slice: x: 2, y: 2, z: 4, core: 2. Of those that a mesh axis runs over, the one named last changes fastest.
Arguments:
- coeffs: bfloat16 [120, 16, 256, 256], P('harm', 'space'), may hold values from -6 to 6
- synthesis: bfloat16 [256, 120], replicated, may hold values from -0.5 to 0.5
- projection: bfloat16 [120, 256], replicated, may hold values from -0.375 to 0.375
- turn_projection: bfloat16 [3, 120, 256], replicated, may hold values from -0.375 to 0.375
- damping: float32 [120], replicated, may hold values from 0.2 to 2
Outputs:
- rate: bfloat16 [120, 16, 256, 256], P('harm', 'space')
- velocity: float32 [3, 16, 256, 256], P(None, 'space', 'harm')
The draws below stay inside these ranges and needn't reach their ends.
All inputs are finite; a program needn't handle non-finite values.
Results may differ from the reference program's by a relative error of at most 0.0042.
Values may be sent and summed in bfloat16 or wider, within the bound.
A program may use at most 192 MiB of HBM per device.

```python
import math
import jax
import jax.numpy as jnp
from jax import lax

NX = 256
NY = 256
COEFS = 120
QUAD = 256
NZ = 16


def levels(own_key, extent, shards, smallest, high):
    factor_of, own = 1.0, jax.random.fold_in(own_key, 6)
    for dim, parts in shards:
        draws = jnp.exp(jax.random.uniform(jax.random.fold_in(own, dim), (parts,), jnp.float32, smallest / len(shards), high / len(shards)))
        factor_of = factor_of * jnp.repeat(draws, extent[dim] // parts).reshape([-1 if axis == dim else 1 for axis in range(len(extent))])
    return factor_of


def noise(stream_key, extent, deviation, limit, shards=(), held_as=jnp.bfloat16):
    loudness = levels(stream_key, extent, shards, -0.22, 0.18) if shards else 1.0
    values = jax.random.normal(stream_key, extent, jnp.float32) * deviation * loudness
    return jnp.minimum(jnp.maximum(values, -limit), limit).astype(held_as)


def setup_inputs(seed: int = 0) -> dict:
    streams_of = jax.random.split(jax.random.key(seed), 6)
    coeffs = noise(streams_of[0], (COEFS, NZ, NY, NX), 1.0, 6.0, ((0, 2), (1, 16)))
    synthesis = noise(streams_of[1], (QUAD, COEFS), COEFS ** -0.5, 0.5)
    projection = noise(streams_of[2], (COEFS, QUAD), QUAD ** -0.5, 0.375)
    turn_projection = noise(streams_of[3], (3, COEFS, QUAD), QUAD ** -0.5, 0.375)
    damping = jnp.clip(jnp.exp(jax.random.uniform(streams_of[4], (COEFS,), jnp.float32, math.log(0.2), math.log(2.0))), 0.2, 2.0)
    return {"coeffs": coeffs, "synthesis": synthesis, "projection": projection, "turn_projection": turn_projection, "damping": damping}


activity = -3.0
swim_speed = 1.0
transl_diff = 0.25
shape_factor = 0.9
golden_angle = math.pi * (3.0 - math.sqrt(5.0))
stress_pairs = ((0, 3, 4), (3, 1, 5), (4, 5, 2))

def sphere_directions(count):
    position = jnp.arange(count, dtype=jnp.float32)
    height = 1.0 - (2.0 * position + 1.0) / count
    radius = jnp.sqrt(1.0 - height * height)
    turning = position * golden_angle
    return jnp.stack([radius * jnp.cos(turning), radius * jnp.sin(turning), height])

def moment_table(synthesis, directions):
    dir_x, dir_y, dir_z = (directions[0], directions[1], directions[2])
    third = 1.0 / 3.0
    moments = jnp.stack([dir_x * dir_x - third, dir_y * dir_y - third, dir_z * dir_z - third, dir_x * dir_y, dir_x * dir_z, dir_y * dir_z])
    table = jnp.dot(moments, synthesis.astype(jnp.float32), precision=lax.Precision.HIGHEST)
    return (table * (activity / math.sqrt(synthesis.shape[0]))).astype(jnp.bfloat16)

def signed_wave(position, length):
    signed = jnp.where(position < length // 2, position, position - length)
    signed = jnp.where(position == length // 2, 0, signed)
    return 2.0 * math.pi / length * signed.astype(jnp.float32)

def differences(center, lower_z, upper_z, lower_y, upper_y):
    middle = center.astype(jnp.float32)
    upper_x = jnp.roll(middle, -1, 3)
    lower_x = jnp.roll(middle, 1, 3)
    lower_y = lower_y.astype(jnp.float32)
    upper_y = upper_y.astype(jnp.float32)
    lower_z = lower_z.astype(jnp.float32)
    upper_z = upper_z.astype(jnp.float32)
    gradients = ((0.5 * (upper_x - lower_x)).astype(jnp.bfloat16), (0.5 * (upper_y - lower_y)).astype(jnp.bfloat16), (0.5 * (upper_z - lower_z)).astype(jnp.bfloat16))
    laplacian = (upper_x + lower_x + upper_y + lower_y + upper_z + lower_z - 6.0 * middle).astype(jnp.bfloat16)
    return (gradients, laplacian)

def orient_rates(coef_block, gradients, laplacian, flow, directions, synthesis, projection, turn_projection, damping):
    density = jnp.dot(synthesis, coef_block, preferred_element_type=jnp.float32)
    advection = jnp.zeros_like(density)
    for j in range(3):
        slope = jnp.dot(synthesis, gradients[j], preferred_element_type=jnp.float32)
        advection = advection - (swim_speed * directions[j][:, None] + flow[j][None, :]) * slope
    strained = []
    for i in range(3):
        total = jnp.zeros_like(density)
        for j in range(3):
            forward_term = flow[3 + 3 * i + j]
            mirror_term = flow[3 + 3 * j + i]
            coupling = 0.5 * shape_factor * (forward_term + mirror_term) + 0.5 * (forward_term - mirror_term)
            total = total + coupling[None, :] * directions[j][:, None]
        strained.append(total)
    radial = directions[0][:, None] * strained[0] + directions[1][:, None] * strained[1] + directions[2][:, None] * strained[2]
    result = jnp.dot(projection, advection.astype(jnp.bfloat16), preferred_element_type=jnp.float32)
    for k in range(3):
        twist = ((strained[k] - directions[k][:, None] * radial) * density).astype(jnp.bfloat16)
        result = result + jnp.dot(turn_projection[k], twist, preferred_element_type=jnp.float32)
    result = result + transl_diff * laplacian.astype(jnp.float32) - damping[:, None] * coef_block.astype(jnp.float32)
    return result.astype(jnp.bfloat16)

def cell_rates(flat_coefs, flat_grads, flat_lap, flat_flow, directions, synthesis, projection, turn_projection, damping):
    cell_count = flat_coefs.shape[1]
    block_len = min(2048, cell_count)

    def advance(block_index, rate_cells):
        offset = block_index * block_len

        def window(array):
            return lax.dynamic_slice_in_dim(array, offset, block_len, 1)
        result = orient_rates(window(flat_coefs), tuple((window(g) for g in flat_grads)), window(flat_lap), window(flat_flow), directions, synthesis, projection, turn_projection, damping)
        return lax.dynamic_update_slice_in_dim(rate_cells, result, offset, 1)
    empty = jnp.zeros(flat_coefs.shape, jnp.bfloat16)
    return lax.fori_loop(0, cell_count // block_len, advance, empty)

def reference(coeffs, synthesis, projection, turn_projection, damping):
    directions = sphere_directions(QUAD)
    table = moment_table(synthesis, directions)
    stress = jnp.dot(table, coeffs.reshape(COEFS, -1), preferred_element_type=jnp.float32).reshape(6, NZ, NY, NX)
    spectrum = jnp.fft.fftn(stress, axes=(1, 2, 3))
    wave_x = signed_wave(jnp.arange(NX, dtype=jnp.int32), NX)[None, None, :]
    wave_y = signed_wave(jnp.arange(NY, dtype=jnp.int32), NY)[None, :, None]
    wave_z = signed_wave(jnp.arange(NZ, dtype=jnp.int32), NZ)[:, None, None]
    wave_vec = (wave_x, wave_y, wave_z)
    wave_sq = wave_x * wave_x + wave_y * wave_y + wave_z * wave_z
    inverse = jnp.where(wave_sq > 0, 1.0 / jnp.where(wave_sq > 0, wave_sq, 1.0), 0.0)
    force = []
    for i in range(3):
        total = spectrum[stress_pairs[i][0]] * wave_vec[0]
        total = total + spectrum[stress_pairs[i][1]] * wave_vec[1]
        total = total + spectrum[stress_pairs[i][2]] * wave_vec[2]
        force.append(1j * total)
    along = wave_vec[0] * force[0] + wave_vec[1] * force[1] + wave_vec[2] * force[2]
    flow_hat = [(force[i] - wave_vec[i] * along * inverse) * inverse for i in range(3)]
    pieces = list(flow_hat)
    for i in range(3):
        for j in range(3):
            pieces.append(1j * wave_vec[j] * flow_hat[i])
    fields = jnp.real(jnp.fft.ifftn(jnp.stack(pieces), axes=(1, 2, 3))).astype(jnp.float32)

    def one_plane(plane):
        center = lax.dynamic_index_in_dim(coeffs, plane, 1, True)
        lower_z = lax.dynamic_index_in_dim(coeffs, (plane + NZ - 1) % NZ, 1, True)
        upper_z = lax.dynamic_index_in_dim(coeffs, (plane + 1) % NZ, 1, True)
        gradients, laplacian = differences(center, lower_z, upper_z, jnp.roll(center, 1, 2), jnp.roll(center, -1, 2))
        flow = lax.dynamic_index_in_dim(fields, plane, 1, True).reshape(12, -1)
        return cell_rates(center.reshape(COEFS, -1), tuple((g.reshape(COEFS, -1) for g in gradients)), laplacian.reshape(COEFS, -1), flow, directions, synthesis, projection, turn_projection, damping)
    stacked = lax.map(one_plane, jnp.arange(NZ, dtype=jnp.int32))
    rate = jnp.transpose(stacked, (1, 0, 2)).reshape(COEFS, NZ, NY, NX)
    return (rate, fields[0:3])
```

```python
import functools
import math

import jax
import jax.numpy as jnp
from jax import lax
from jax.experimental import pallas as pl
from jax.experimental.pallas import tpu as pltpu
from jax.sharding import PartitionSpec as P

activity = -3.0
swim_speed = 1.0
transl_diff = 0.25
shape_factor = 0.9
golden_angle = math.pi * (3.0 - math.sqrt(5.0))
stress_pairs = ((0, 3, 4), (3, 1, 5), (4, 5, 2))
chunk = 16
MESH = pl.DeviceIdType.MESH
VMEM_BYTES = 66_000_000


def sphere_directions(count):
    position = jnp.arange(count, dtype=jnp.float32)
    height = 1.0 - (2.0 * position + 1.0) / count
    radius = jnp.sqrt(1.0 - height * height)
    turning = position * golden_angle
    return jnp.stack([radius * jnp.cos(turning), radius * jnp.sin(turning), height])


def moment_table(synthesis, directions):
    dir_x, dir_y, dir_z = (directions[0], directions[1], directions[2])
    third = 1.0 / 3.0
    moments = jnp.stack(
        [
            dir_x * dir_x - third,
            dir_y * dir_y - third,
            dir_z * dir_z - third,
            dir_x * dir_y,
            dir_x * dir_z,
            dir_y * dir_z,
        ]
    )
    table = jnp.dot(moments, synthesis.astype(jnp.float32), precision=lax.Precision.HIGHEST)
    return (table * (activity / math.sqrt(synthesis.shape[0]))).astype(jnp.bfloat16)


def signed_wave(position, length):
    signed = jnp.where(position < length // 2, position, position - length)
    signed = jnp.where(position == length // 2, 0, signed)
    return 2.0 * math.pi / length * signed.astype(jnp.float32)


def dft_tables(length, frequency):
    phase = jnp.arange(length, dtype=jnp.int32)[:, None] * frequency[None, :] % length
    angle = phase.astype(jnp.float32) * (2.0 * math.pi / length)
    return (jnp.cos(angle), jnp.sin(angle))


def composite_tables(directions, synthesis, projection, turn_projection):
    def through(weights):
        return jnp.dot(weights, synthesis.astype(jnp.float32), precision=lax.Precision.HIGHEST)

    project = projection.astype(jnp.float32)
    turning = turn_projection.astype(jnp.float32)
    radial = sum(turning[k] * directions[k] for k in range(3))
    tables = [through(-swim_speed * project * directions[j]) for j in range(3)]
    tables.append(through(-project))
    strain = [
        [through((turning[i] - radial * directions[i]) * directions[j]) for j in range(3)]
        for i in range(3)
    ]
    for i in range(3):
        for j in range(3):
            if i + j < 4:
                tables.append(strain[i][j] - strain[2][2] if i == j else strain[i][j])
    stacked = jnp.stack(tables, axis=1)
    coefs = stacked.shape[2]
    stacked = jnp.pad(stacked, ((0, 0), (0, 0), (0, -coefs % 16)))
    return stacked.astype(jnp.bfloat16).reshape(stacked.shape[0], -1)


def stokes_fields(stress, spaces, groups, space_id, group_id):
    highest = lax.Precision.HIGH
    length_x = stress.shape[3]
    packed = (length_x // 2) % (spaces * groups) == 0
    slots = length_x // 2 if packed else length_x
    cos_x, sin_x = dft_tables(length_x, jnp.arange(slots, dtype=jnp.int32))
    parity = 1.0 - 2.0 * (jnp.arange(length_x, dtype=jnp.int32) % 2).astype(jnp.float32)
    sin_x = -sin_x
    if packed:
        sin_x = sin_x.at[:, 0].set(parity)
    real_part = jnp.einsum("abcn,nm->ambc", stress, cos_x, precision=highest)
    imag_part = jnp.einsum("abcn,nm->ambc", stress, sin_x, precision=highest)
    columns = lax.all_to_all(
        lax.all_to_all(
            jnp.stack([real_part, imag_part]).astype(jnp.bfloat16), "space", split_axis=2, concat_axis=3, tiled=True
        ),
        "harm",
        split_axis=2,
        concat_axis=4,
        tiled=True,
    )
    columns = columns.astype(jnp.float32)
    real_part, imag_part = (columns[0], columns[1])
    columns_dev = columns.shape[2]
    length_z = columns.shape[3]
    length_y = columns.shape[4]
    cos_y, sin_y = dft_tables(length_y, jnp.arange(length_y, dtype=jnp.int32))
    cos_z, sin_z = dft_tables(length_z, jnp.arange(length_z, dtype=jnp.int32))
    real_next = jnp.einsum("ajzn,nm->ajzm", real_part, cos_y, precision=highest) + jnp.einsum(
        "ajzn,nm->ajzm", imag_part, sin_y, precision=highest
    )
    imag_next = jnp.einsum("ajzn,nm->ajzm", imag_part, cos_y, precision=highest) - jnp.einsum(
        "ajzn,nm->ajzm", real_part, sin_y, precision=highest
    )
    real_part = jnp.einsum("ajny,nm->ajmy", real_next, cos_z, precision=highest) + jnp.einsum(
        "ajny,nm->ajmy", imag_next, sin_z, precision=highest
    )
    imag_part = jnp.einsum("ajny,nm->ajmy", imag_next, cos_z, precision=highest) - jnp.einsum(
        "ajny,nm->ajmy", real_next, sin_z, precision=highest
    )
    column_freq = (
        space_id * groups * columns_dev
        + group_id * columns_dev
        + jnp.arange(columns_dev, dtype=jnp.int32)
    )
    wave_x = signed_wave(column_freq, length_x)[:, None, None]
    wave_y = signed_wave(jnp.arange(length_y, dtype=jnp.int32), length_y)[None, None, :]
    wave_z = signed_wave(jnp.arange(length_z, dtype=jnp.int32), length_z)[None, :, None]
    wave_vec = (wave_x, wave_y, wave_z)
    wave_sq = wave_x * wave_x + wave_y * wave_y + wave_z * wave_z
    inverse = jnp.where(wave_sq > 0, 1.0 / jnp.where(wave_sq > 0, wave_sq, 1.0), 0.0)
    force_real = []
    force_imag = []
    for i in range(3):
        sum_real = (
            real_part[stress_pairs[i][0]] * wave_vec[0]
            + real_part[stress_pairs[i][1]] * wave_vec[1]
            + real_part[stress_pairs[i][2]] * wave_vec[2]
        )
        sum_imag = (
            imag_part[stress_pairs[i][0]] * wave_vec[0]
            + imag_part[stress_pairs[i][1]] * wave_vec[1]
            + imag_part[stress_pairs[i][2]] * wave_vec[2]
        )
        force_real.append(-sum_imag)
        force_imag.append(sum_real)
    along_real = (
        wave_vec[0] * force_real[0] + wave_vec[1] * force_real[1] + wave_vec[2] * force_real[2]
    )
    along_imag = (
        wave_vec[0] * force_imag[0] + wave_vec[1] * force_imag[1] + wave_vec[2] * force_imag[2]
    )
    flow_real = [(force_real[i] - wave_vec[i] * along_real * inverse) * inverse for i in range(3)]
    flow_imag = [(force_imag[i] - wave_vec[i] * along_imag * inverse) * inverse for i in range(3)]
    pieces_real = list(flow_real)
    pieces_imag = list(flow_imag)
    for i in range(3):
        for j in range(1, 3 if i < 2 else 2):
            pieces_real.append(-wave_vec[j] * flow_imag[i])
            pieces_imag.append(wave_vec[j] * flow_real[i])
    real_part = jnp.stack(pieces_real)
    imag_part = jnp.stack(pieces_imag)
    real_next = jnp.einsum("ajny,nm->ajmy", real_part, cos_z, precision=highest) - jnp.einsum(
        "ajny,nm->ajmy", imag_part, sin_z, precision=highest
    )
    imag_next = jnp.einsum("ajny,nm->ajmy", imag_part, cos_z, precision=highest) + jnp.einsum(
        "ajny,nm->ajmy", real_part, sin_z, precision=highest
    )
    real_part = jnp.einsum("ajzn,nm->ajzm", real_next, cos_y, precision=highest) - jnp.einsum(
        "ajzn,nm->ajzm", imag_next, sin_y, precision=highest
    )
    imag_part = jnp.einsum("ajzn,nm->ajzm", imag_next, cos_y, precision=highest) + jnp.einsum(
        "ajzn,nm->ajzm", real_next, sin_y, precision=highest
    )
    returned = lax.all_to_all(
        lax.all_to_all(
            jnp.stack([real_part, imag_part]).astype(jnp.bfloat16), "space", split_axis=3, concat_axis=2, tiled=True
        ),
        "harm",
        split_axis=4,
        concat_axis=2,
        tiled=True,
    )
    returned = returned.astype(jnp.float32)
    position = jnp.arange(slots, dtype=jnp.int32)
    owner_group = position // (spaces * columns_dev)
    owner_space = position // columns_dev % spaces
    owner_column = position % columns_dev
    return_freq = owner_space * groups * columns_dev + owner_group * columns_dev + owner_column
    cos_back, sin_back = dft_tables(length_x, return_freq)
    from_real, from_imag = cos_back, -sin_back
    if packed:
        first = (return_freq == 0)[None, :]
        from_real = jnp.where(first, 1.0, 2.0 * from_real)
        from_imag = jnp.where(first, parity[:, None], 2.0 * from_imag)
    scale = 1.0 / (length_x * length_y * length_z)
    from_real, from_imag = from_real * scale, from_imag * scale
    wave_back = signed_wave(return_freq, length_x)[None, :]

    def back(pieces_real, pieces_imag, table_real, table_imag):
        return jnp.einsum("akbc,nk->abcn", pieces_real, table_real, precision=highest) + jnp.einsum(
            "akbc,nk->abcn", pieces_imag, table_imag, precision=highest
        )

    plain = back(returned[0], returned[1], from_real, from_imag)
    along_x = back(returned[0, :3], returned[1, :3], wave_back * from_imag, -wave_back * from_real)
    velocity, others = plain[:3], plain[3:]
    trace_rest = -(along_x[0] + others[2])
    return jnp.stack(
        [
            velocity[0],
            velocity[1],
            velocity[2],
            along_x[0],
            others[0],
            others[1],
            along_x[1],
            others[2],
            others[3],
            along_x[2],
            others[4],
            trace_rest,
        ]
    )


def greet(partners):
    barrier = pltpu.get_barrier_semaphore()
    for partner in partners:
        pl.semaphore_signal(barrier, inc=1, device_id=partner, device_id_type=MESH)
    pl.semaphore_wait(barrier, len(partners))


def ring_partners(spaces, groups):
    space_id, group_id = lax.axis_index("space"), lax.axis_index("harm")
    upper = (lax.rem(space_id + 1, spaces), group_id)
    lower = (lax.rem(space_id + spaces - 1, spaces), group_id)
    others = [(space_id, lax.rem(group_id + o, groups)) for o in range(1, groups)]
    return space_id, group_id, lower, upper, others


def exchange_kernel(
    spaces, groups, coeffs, edges, mid, below, above, edges_in, mid_send, mid_recv, halo_send, halo_recv, edge_send, edge_recv
):
    space_id, group_id, lower, upper, others = ring_partners(spaces, groups)
    rows = mid.shape[2]
    steps = rows // chunk
    greet([lower, upper] + others)

    def strip(group, step):
        return pl.ds(pl.multiple_of(group * rows + step * chunk, chunk), chunk)

    def regroup(step, o):
        _, target = others[o]
        return pltpu.make_async_remote_copy(
            src_ref=coeffs.at[:, 0, strip(target, step)],
            dst_ref=mid.at[groups - 2 - o, :, pl.ds(pl.multiple_of(step * chunk, chunk), chunk)],
            send_sem=mid_send.at[o, step],
            recv_sem=mid_recv.at[groups - 2 - o, step],
            device_id=others[o],
            device_id_type=MESH,
        )

    def halo(step, side):
        return pltpu.make_async_remote_copy(
            src_ref=coeffs.at[:, 0, strip(group_id, step)],
            dst_ref=(above if side == 0 else below).at[:, pl.ds(pl.multiple_of(step * chunk, chunk), chunk)],
            send_sem=halo_send.at[side, step],
            recv_sem=halo_recv.at[side, step],
            device_id=lower if side == 0 else upper,
            device_id_type=MESH,
        )

    def edge(o):
        return pltpu.make_async_remote_copy(
            src_ref=edges.at[others[o][1]],
            dst_ref=edges_in.at[group_id],
            send_sem=edge_send.at[o],
            recv_sem=edge_recv.at[groups - 2 - o],
            device_id=others[o],
            device_id_type=MESH,
        )

    for o in range(groups - 1):
        edge(o).start()

    @pl.loop(0, steps)
    def _(step):
        for o in range(groups - 1):
            regroup(step, o).start()
        halo(step, 0).start()
        halo(step, 1).start()

    edges_in[group_id] = edges[group_id]

    @pl.loop(0, steps)
    def _(step):
        for o in range(groups - 1):
            regroup(step, o).wait()
        halo(step, 0).wait()
        halo(step, 1).wait()

    for o in range(groups - 1):
        edge(o).wait()


def exchange(coeffs, edges, spaces, groups):
    coefs, _, length_y, length_x = coeffs.shape
    rows = length_y // groups
    steps = rows // chunk
    anywhere = pl.BlockSpec(memory_space=pl.ANY)
    vmem = pl.BlockSpec(memory_space=pltpu.VMEM)
    strip = jax.ShapeDtypeStruct((coefs, rows, length_x), coeffs.dtype)
    return pl.pallas_call(
        functools.partial(exchange_kernel, spaces, groups),
        out_shape=(
            jax.ShapeDtypeStruct((groups - 1, coefs, rows, length_x), coeffs.dtype),
            strip,
            strip,
            jax.ShapeDtypeStruct(edges.shape, edges.dtype),
        ),
        in_specs=[anywhere, vmem],
        out_specs=(anywhere, anywhere, anywhere, vmem),
        scratch_shapes=[
            pltpu.SemaphoreType.DMA((groups - 1, steps)),
            pltpu.SemaphoreType.DMA((groups - 1, steps)),
            pltpu.SemaphoreType.DMA((2, steps)),
            pltpu.SemaphoreType.DMA((2, steps)),
            pltpu.SemaphoreType.DMA((groups - 1,)),
            pltpu.SemaphoreType.DMA((groups - 1,)),
        ],
        compiler_params=pltpu.CompilerParams(collective_id=0, has_side_effects=True),
    )(coeffs, edges)


def rate_kernel(
    spaces,
    groups,
    coeffs,
    mid,
    below,
    above,
    edges,
    flow,
    tables,
    decay,
    shifts,
    rate,
    lines,
    mid_part,
    below_part,
    above_part,
    below_far,
    above_far,
    flat,
    slope_x,
    smooth,
    inputs,
    stage,
    far_send,
    far_recv,
    load_sem,
    out_send,
    out_recv,
    own_sem,
):
    space_id, group_id, lower, upper, others = ring_partners(spaces, groups)
    coefs, _, _, length_x = coeffs.shape
    rows = mid.shape[2]
    steps = rows // chunk
    total = groups * coefs
    padded = lines.shape[1]
    greet([lower, upper] + others)

    def part(step):
        return pl.ds(pl.multiple_of(step * chunk, chunk), chunk)

    def far(step, side):
        return pltpu.make_async_remote_copy(
            src_ref=mid.at[:, :, part(step)],
            dst_ref=(above_far if side == 0 else below_far).at[:, :, part(step)],
            send_sem=far_send.at[side, step],
            recv_sem=far_recv.at[side, step],
            device_id=lower if side == 0 else upper,
            device_id_type=MESH,
        )

    own_rows = group_id * rows

    def mid_loads(step):
        slot = lax.rem(step, 2)
        own = pltpu.make_async_copy(
            coeffs.at[:, 0, pl.ds(pl.multiple_of(own_rows + step * chunk, chunk), chunk)],
            mid_part.at[slot, pl.ds(group_id * coefs, coefs)],
            load_sem.at[slot, 0],
        )
        rest = [
            pltpu.make_async_copy(
                mid.at[o, :, part(step)],
                mid_part.at[slot, pl.ds(others[o][1] * coefs, coefs)],
                load_sem.at[slot, 3 + o],
            )
            for o in range(groups - 1)
        ]
        return [own] + rest

    def halo_loads(step):
        slot = lax.rem(step, 2)
        return [
            pltpu.make_async_copy(below.at[:, part(step)], below_part.at[slot], load_sem.at[slot, 1]),
            pltpu.make_async_copy(above.at[:, part(step)], above_part.at[slot], load_sem.at[slot, 2]),
        ]

    @pl.loop(0, steps)
    def _(step):
        far(step, 0).start()
        far(step, 1).start()

    for copy in mid_loads(0) + halo_loads(0):
        copy.start()

    lines[0] = edges[0]
    lines[rows + 1] = edges[1]
    lanes = 128
    halves_x = length_x // lanes
    zeros = jnp.zeros((padded - total, length_x), jnp.float32)

    def columns(row):
        values = jnp.concatenate(
            [flat[half, pl.ds(row, total, stride=chunk), :] for half in range(halves_x)], axis=1
        )
        return jnp.concatenate([values, zeros], axis=0) if padded > total else values

    def transpose_mid(step):
        for copy in mid_loads(step):
            copy.wait()
        slot = lax.rem(step, 2)
        for half in range(halves_x):
            cut = slice(half * lanes, (half + 1) * lanes)
            flat[half] = mid_part[slot, :, :, cut].astype(jnp.float32).reshape(total * chunk, lanes)
        for row in range(chunk):
            lines[step * chunk + 1 + row] = columns(row).astype(jnp.bfloat16)

    def out_copies(step):
        slot = lax.rem(step, 2)
        place = pl.ds(pl.multiple_of(own_rows + step * chunk, chunk), chunk)
        own = pltpu.make_async_copy(
            stage.at[slot, pl.ds(group_id * coefs, coefs)], rate.at[:, 0, place], own_sem.at[slot]
        )
        rest = [
            pltpu.make_async_remote_copy(
                src_ref=stage.at[slot, pl.ds(others[o][1] * coefs, coefs)],
                dst_ref=rate.at[:, 0, place],
                send_sem=out_send.at[o, step],
                recv_sem=out_recv.at[groups - 2 - o, step],
                device_id=others[o],
                device_id_type=MESH,
            )
            for o in range(groups - 1)
        ]
        return own, rest

    transpose_mid(0)

    @pl.loop(0, steps)
    def _(step):
        slot = lax.rem(step, 2)

        @pl.when(step + 1 < steps)
        def _():
            for copy in mid_loads(step + 1) + halo_loads(step + 1):
                copy.start()

        start = pl.multiple_of(step * chunk, chunk)
        block = lines[pl.ds(start + 1, chunk)].reshape(chunk * padded, length_x)
        slope_x[...] = jnp.dot(block, shifts[0], preferred_element_type=jnp.float32).astype(jnp.bfloat16)
        smooth[...] = jnp.dot(block, shifts[1], preferred_element_type=jnp.float32)

        @pl.when(step + 1 < steps)
        def _():
            transpose_mid(step + 1)

        for copy in halo_loads(step):
            copy.wait()
        far(step, 0).wait_recv()
        far(step, 1).wait_recv()

        def halves(o):
            if o < 0:
                return group_id, below_part[slot].astype(jnp.float32), above_part[slot].astype(jnp.float32)
            return (
                others[o][1],
                below_far[o, :, part(step)].astype(jnp.float32),
                above_far[o, :, part(step)].astype(jnp.float32),
            )

        size = coefs * chunk
        for o in range(-1, groups - 1):
            group, low, high = halves(o)
            for half in range(halves_x):
                cut = slice(half * lanes, (half + 1) * lanes)
                slope = 0.5 * (high[:, :, cut] - low[:, :, cut])
                flat[half, pl.ds(pl.multiple_of(group * size, 8), size), :] = slope.reshape(size, lanes)

        def one_row(row):
            line = start + 1 + row
            center = lines[line]
            high_y = lines[line + 1].astype(jnp.float32)
            low_y = lines[line - 1].astype(jnp.float32)
            at = pl.ds(pl.multiple_of(row * padded, padded), padded)
            slope_z = columns(row)
            slope_y = 0.5 * (high_y - low_y)
            first = slope_x[at, :]
            here = start + row

            def field(i):
                return flow[i, pl.ds(here, 1), :]

            inputs[0:padded] = first
            inputs[padded : 2 * padded] = slope_y.astype(jnp.bfloat16)
            inputs[2 * padded : 3 * padded] = slope_z.astype(jnp.bfloat16)
            carried = field(0) * first.astype(jnp.float32) + field(1) * slope_y + field(2) * slope_z
            inputs[3 * padded : 4 * padded] = carried.astype(jnp.bfloat16)
            for i in range(8):
                inputs[(4 + i) * padded : (5 + i) * padded] = center * field(3 + i).astype(jnp.bfloat16)
            result = jnp.dot(tables[...], inputs[...], preferred_element_type=jnp.float32)
            result = result + smooth[at, :] + transl_diff * (high_y + low_y)
            result = result - decay[...] * center.astype(jnp.float32)
            smooth[at, :] = result

        @pl.loop(0, chunk)
        def _(row):
            one_row(row)

        for row in range(chunk):
            for half in range(halves_x):
                cut = slice(half * lanes, (half + 1) * lanes)
                flat[half, pl.ds(row, total, stride=chunk), :] = smooth[pl.ds(row * padded, total), cut]

        @pl.when(step >= 2)
        def _():
            own, rest = out_copies(step - 2)
            own.wait()
            for copy in rest:
                copy.wait_send()

        for o in range(-1, groups - 1):
            group, low, high = halves(o)
            for half in range(halves_x):
                cut = slice(half * lanes, (half + 1) * lanes)
                value = flat[half, pl.ds(pl.multiple_of(group * size, 8), size), :].reshape(coefs, chunk, lanes)
                value = value + transl_diff * (high[:, :, cut] + low[:, :, cut])
                stage[slot, pl.ds(group * coefs, coefs), :, cut] = value.astype(jnp.bfloat16)
        own, rest = out_copies(step)
        own.start()
        for copy in rest:
            copy.start()

    for step in range(max(steps - 2, 0), steps):
        own, rest = out_copies(step)
        own.wait()
        for copy in rest:
            copy.wait_send()

    @pl.loop(0, steps)
    def _(step):
        far(step, 0).wait_send()
        far(step, 1).wait_send()
        for copy in out_copies(step)[1]:
            copy.wait_recv()


def rates(coeffs, mid, below, above, edges, flow, tables, decay, shifts, spaces, groups):
    coefs, _, length_y, length_x = coeffs.shape
    rows = length_y // groups
    steps = rows // chunk
    total = groups * coefs
    padded = tables.shape[0]
    anywhere = pl.BlockSpec(memory_space=pl.ANY)
    vmem = pl.BlockSpec(memory_space=pltpu.VMEM)
    kept = coeffs.dtype
    return pl.pallas_call(
        functools.partial(rate_kernel, spaces, groups),
        out_shape=jax.ShapeDtypeStruct(coeffs.shape, kept),
        in_specs=[anywhere] * 4 + [vmem] * 5,
        out_specs=anywhere,
        scratch_shapes=[
            pltpu.VMEM((rows + 2, padded, length_x), kept),
            pltpu.VMEM((2, total, chunk, length_x), kept),
            pltpu.VMEM((2, coefs, chunk, length_x), kept),
            pltpu.VMEM((2, coefs, chunk, length_x), kept),
            pltpu.VMEM((groups - 1, coefs, rows, length_x), kept),
            pltpu.VMEM((groups - 1, coefs, rows, length_x), kept),
            pltpu.VMEM((length_x // 128, total * chunk, 128), jnp.float32),
            pltpu.VMEM((chunk * padded, length_x), kept),
            pltpu.VMEM((chunk * padded, length_x), jnp.float32),
            pltpu.VMEM((tables.shape[1], length_x), kept),
            pltpu.VMEM((2, total, chunk, length_x), kept),
            pltpu.SemaphoreType.DMA((2, steps)),
            pltpu.SemaphoreType.DMA((2, steps)),
            pltpu.SemaphoreType.DMA((2, groups + 2)),
            pltpu.SemaphoreType.DMA((groups - 1, steps)),
            pltpu.SemaphoreType.DMA((groups - 1, steps)),
            pltpu.SemaphoreType.DMA((2,)),
        ],
        compiler_params=pltpu.CompilerParams(
            collective_id=1, has_side_effects=True, vmem_limit_bytes=VMEM_BYTES
        ),
    )(coeffs, mid, below, above, edges, flow, tables, decay, shifts)


def shift_tables(length):
    eye = jnp.eye(length, dtype=jnp.float32)
    after, before = jnp.roll(eye, 1, 0), jnp.roll(eye, -1, 0)
    slope = 0.5 * (after - before)
    around = transl_diff * (after + before)
    return jnp.stack([slope, around]).astype(jnp.bfloat16)


def couplings(fields):
    found = [fields[0], fields[1], fields[2]]
    for i in range(3):
        for j in range(3):
            if i + j < 4:
                forward_term, mirror_term = fields[3 + 3 * i + j], fields[3 + 3 * j + i]
                found.append(
                    0.5 * shape_factor * (forward_term + mirror_term)
                    + 0.5 * (forward_term - mirror_term)
                )
    return jnp.stack(found)


def boundary_rows(coeffs, groups):
    rows = coeffs.shape[2] // groups
    found = []
    for group in range(groups):
        for row in ((group * rows - 1) % (groups * rows), (group + 1) * rows % (groups * rows)):
            found.append(coeffs[:, 0, row])
    return jnp.stack(found).reshape(groups, 2, coeffs.shape[0], coeffs.shape[3])


def local(coeffs, synthesis, projection, turn_projection, damping):
    spaces = lax.axis_size("space")
    groups = lax.axis_size("harm")
    space_id = lax.axis_index("space")
    group_id = lax.axis_index("harm")
    local_coefs, planes, length_y, length_x = coeffs.shape
    total_coefs = synthesis.shape[1]
    directions = sphere_directions(synthesis.shape[0])
    table = moment_table(synthesis, directions)
    mid, below, above, edges_in = exchange(coeffs, boundary_rows(coeffs, groups), spaces, groups)
    own_table = lax.dynamic_slice_in_dim(table, group_id * local_coefs, local_coefs, 1)
    partial_stress = jnp.dot(
        own_table, coeffs.reshape(local_coefs, -1), preferred_element_type=jnp.float32
    )
    partial_stress = partial_stress.reshape(6, planes, length_y, length_x)
    stress = lax.psum_scatter(partial_stress, "harm", scatter_dimension=2, tiled=True)
    fields = stokes_fields(stress, spaces, groups, space_id, group_id)
    tables = composite_tables(directions, synthesis, projection, turn_projection)
    padded = tables.shape[1] // 12
    extra = padded - total_coefs
    tables = jnp.pad(tables, ((0, extra), (0, 0)))
    decay = jnp.pad(damping + 6.0 * transl_diff, (0, extra))
    decay = jnp.broadcast_to(decay[:, None], (padded, length_x))
    edges = edges_in.transpose(1, 0, 2, 3).reshape(2, total_coefs, length_x)
    edges = jnp.pad(edges, ((0, 0), (0, extra), (0, 0)))
    flow = couplings(fields).reshape(11, -1, length_x)
    rate = rates(
        coeffs, mid, below, above, edges, flow, tables, decay, shift_tables(length_x), spaces, groups
    )
    return (rate, fields[0:3])


def solution(mesh):
    in_specs = (P("harm", "space", None, None), P(), P(), P(), P())
    out_specs = (P("harm", "space", None, None), P(None, "space", "harm", None))
    return jax.shard_map(local, mesh=mesh, in_specs=in_specs, out_specs=out_specs, check_vma=False)
```

```python
import functools
import math

import jax
import jax.numpy as jnp
import numpy as np
from jax import lax
from jax.experimental import pallas as pl
from jax.experimental.pallas import tpu as pltpu
from jax.sharding import PartitionSpec as P

activity = -3.0
swim_speed = 1.0
transl_diff = 0.25
shape_factor = 0.9
golden_angle = math.pi * (3.0 - math.sqrt(5.0))
chunk = 16
MESH = pl.DeviceIdType.MESH
VMEM_BYTES = 66_000_000
lead, second, ahead = 2, 4, 1


def sphere_directions(count):
    position = np.arange(count)
    height = 1.0 - (2.0 * position + 1.0) / count
    radius = np.sqrt(1.0 - height * height)
    turning = position * golden_angle
    return np.stack([radius * np.cos(turning), radius * np.sin(turning), height])


def moment_table(synthesis):
    count = synthesis.shape[0]
    dir_x, dir_y, dir_z = sphere_directions(count)
    third = 1.0 / 3.0
    moments = np.stack(
        [
            dir_x * dir_x - third,
            dir_y * dir_y - third,
            dir_z * dir_z - third,
            dir_x * dir_y,
            dir_x * dir_z,
            dir_y * dir_z,
        ]
    )
    moments = jnp.asarray(moments, jnp.float32)
    table = jnp.dot(moments, synthesis.astype(jnp.float32), precision=lax.Precision.HIGHEST)
    return (table * (activity / math.sqrt(count))).astype(jnp.bfloat16)


def greet(partners):
    barrier = pltpu.get_barrier_semaphore()
    for partner in partners:
        pl.semaphore_signal(barrier, inc=1, device_id=partner, device_id_type=MESH)
    pl.semaphore_wait(barrier, len(partners))


def ring_partners(spaces, groups):
    space_id, group_id = lax.axis_index("space"), lax.axis_index("harm")
    upper = (lax.rem(space_id + 1, spaces), group_id)
    lower = (lax.rem(space_id + spaces - 1, spaces), group_id)
    others = [(space_id, lax.rem(group_id + o, groups)) for o in range(1, groups)]
    return space_id, group_id, lower, upper, others


def signed_wave(length):
    position = np.arange(length)
    signed = np.where(position < length // 2, position, position - length)
    return 2.0 * np.pi / length * np.where(position == length // 2, 0, signed)


def two_parts(table):
    high = np.asarray(table).astype(jnp.bfloat16)
    low = (table - high.astype(np.float64)).astype(jnp.bfloat16)
    return jnp.asarray(np.stack([high, low]))


def spectral_tables(length_x, length_y, length_z, groups):
    slots = length_x // 2
    place_x, freq_x = np.arange(length_x), np.arange(slots)
    angle = 2.0 * np.pi / length_x * (place_x[:, None] * freq_x[None, :] % length_x)
    cos_x, sin_x = np.cos(angle), np.sin(angle)
    parity = 1.0 - 2.0 * (place_x % 2)
    into_real, into_imag = cos_x, -sin_x
    into_imag[:, 0] = parity
    ahead_x = np.concatenate([into_real, into_imag], axis=1)
    from_real, from_imag = 2.0 * cos_x.T, -2.0 * np.sin(angle).T
    from_real[0], from_imag[0] = 1.0, parity
    scale = 1.0 / (length_x * length_y * length_z)
    wave_x = signed_wave(length_x)[:slots]
    plain = np.concatenate([from_real, from_imag]) * scale
    along = np.concatenate([wave_x[:, None] * from_imag, -wave_x[:, None] * from_real]) * scale
    back_x = np.concatenate([plain, along], axis=1)
    place_y = np.arange(length_y)
    angle = 2.0 * np.pi / length_y * (place_y[:, None] * place_y[None, :] % length_y)
    cos_y, sin_y = np.cos(angle), np.sin(angle)
    wave_y = signed_wave(length_y)
    ahead_y = np.concatenate([cos_y, sin_y])
    back_y = np.stack([cos_y, sin_y, -wave_y * sin_y, wave_y * cos_y])
    back_y = back_y.reshape(4, groups, length_y // groups, length_y).transpose(1, 0, 2, 3)
    back_y = back_y.reshape(groups, -1, length_y)
    place_z = np.arange(length_z)
    angle = 2.0 * np.pi / length_z * (place_z[:, None] * place_z[None, :] % length_z)
    line_z = np.stack([np.cos(angle), np.sin(angle)]).reshape(-1)
    line_z = np.concatenate([line_z, signed_wave(length_z)])
    return (
        jnp.asarray(line_z, jnp.float32),
        two_parts(ahead_x),
        two_parts(ahead_y),
        two_parts(back_y),
        two_parts(back_x),
        jnp.asarray(wave_x[None, :], jnp.float32),
        jnp.asarray(np.broadcast_to(wave_y[:, None], (length_y, slots)), jnp.float32),
    )


def split(values):
    high = values.astype(jnp.bfloat16)
    return high, (values - high.astype(jnp.float32)).astype(jnp.bfloat16)


def dot(left, right):
    return jnp.dot(left, right, preferred_element_type=jnp.float32)


def composite_tables(synthesis, projection, turn_projection, directions, tables):
    total = synthesis.shape[1]
    padded = tables.shape[0]
    tables[...] = jnp.zeros_like(tables)
    basis = synthesis[...]
    project = projection[...].astype(jnp.float32)
    turning = [turn_projection[k].astype(jnp.float32) for k in range(3)]
    along = [directions[k : k + 1, :] for k in range(3)]
    radial = sum(turning[k] * along[k] for k in range(3))

    def strain(i, j):
        return (turning[i] - radial * along[i]) * along[j]

    weights = [-swim_speed * project * along[j] for j in range(3)] + [-project]
    for i in range(3):
        for j in range(3):
            if i + j < 4:
                weights.append(strain(i, j) - strain(2, 2) if i == j else strain(i, j))
    for place, weight in enumerate(weights):
        high, low = split(weight)
        tables[:total, place * padded : place * padded + total] = (
            dot(high, basis) + dot(low, basis)
        ).astype(jnp.bfloat16)


def stokes_kernel(
    spaces,
    groups,
    table,
    line_z,
    coeffs,
    edges,
    ahead_x,
    ahead_y,
    back_y,
    back_x,
    wave_x,
    wave_y,
    synthesis,
    projection,
    turn_projection,
    damping,
    directions,
    mid,
    below,
    above,
    edges_in,
    flow,
    velocity,
    tables,
    decay,
    own,
    stress,
    spectrum,
    send,
    recv,
    planes,
    solved,
    back,
    returned,
    own_sem,
    mid_send,
    mid_recv,
    halo_send,
    halo_recv,
    edge_send,
    edge_recv,
    turn_sem,
):
    space_id, group_id, lower, upper, others = ring_partners(spaces, groups)
    coefs, _, length_y, length_x = coeffs.shape
    rows = mid.shape[2]
    steps = rows // chunk
    count = spaces * groups
    me = space_id * groups + group_id
    owned = length_y // count
    slots = length_x // 2
    message = send.shape[1]

    def own_load(step):
        place = pl.ds(pl.multiple_of(step * chunk, chunk), chunk)
        return pltpu.make_async_copy(coeffs.at[:, 0, place], own.at[:, place], own_sem.at[step])

    @pl.loop(0, length_y // chunk)
    def _(step):
        own_load(step).start()

    barrier = pltpu.get_barrier_semaphore()

    @pl.loop(1, count)
    def _(o):
        other = lax.rem(me + o, count)
        pl.semaphore_signal(
            barrier, inc=1, device_id=(other // groups, lax.rem(other, groups)), device_id_type=MESH
        )

    pl.semaphore_wait(barrier, count - 1)

    def strip(group, step):
        return pl.ds(pl.multiple_of(group * rows + step * chunk, chunk), chunk)

    def regroup(step, o):
        return pltpu.make_async_remote_copy(
            src_ref=coeffs.at[:, 0, strip(others[o][1], step)],
            dst_ref=mid.at[groups - 2 - o, :, pl.ds(pl.multiple_of(step * chunk, chunk), chunk)],
            send_sem=mid_send.at[o, step],
            recv_sem=mid_recv.at[groups - 2 - o, step],
            device_id=others[o],
            device_id_type=MESH,
        )

    def halo(step, side):
        return pltpu.make_async_remote_copy(
            src_ref=coeffs.at[:, 0, strip(group_id, step)],
            dst_ref=(above if side == 0 else below).at[:, pl.ds(pl.multiple_of(step * chunk, chunk), chunk)],
            send_sem=halo_send.at[side, step],
            recv_sem=halo_recv.at[side, step],
            device_id=lower if side == 0 else upper,
            device_id_type=MESH,
        )

    def edge(o):
        return pltpu.make_async_remote_copy(
            src_ref=edges.at[others[o][1]],
            dst_ref=edges_in.at[group_id],
            send_sem=edge_send.at[o],
            recv_sem=edge_recv.at[groups - 2 - o],
            device_id=others[o],
            device_id_type=MESH,
        )

    def bulk(first, last):
        @pl.loop(min(first, steps), min(last, steps))
        def _(step):
            for o in range(groups - 1):
                regroup(step, o).start()
            halo(step, 0).start()
            halo(step, 1).start()

    def turn(source, target, kind, pick):
        @pl.loop(1, count)
        def _(o):
            other = lax.rem(me + o, count)
            pltpu.make_async_remote_copy(
                src_ref=source.at[pick(other)],
                dst_ref=target.at[me],
                send_sem=turn_sem.at[kind, 0],
                recv_sem=turn_sem.at[kind, 1],
                device_id=(other // groups, lax.rem(other, groups)),
                device_id_type=MESH,
            ).start()

    def arrived(target, kind):
        return pltpu.make_async_remote_copy(
            src_ref=target.at[pl.ds(0, count - 1)],
            dst_ref=target.at[pl.ds(0, count - 1)],
            send_sem=turn_sem.at[kind, 0],
            recv_sem=turn_sem.at[kind, 1],
            device_id=upper,
            device_id_type=MESH,
        )

    for o in range(groups - 1):
        edge(o).start()
    bulk(0, lead)
    edges_in[group_id] = edges[group_id]

    @pl.loop(0, length_y // chunk)
    def _(step):
        own_load(step).wait()
        place = pl.ds(pl.multiple_of(step * chunk, chunk), chunk)
        sums = [jnp.zeros((chunk, length_x), jnp.float32) for _ in range(5)]
        for k in range(coefs):
            value = own[k, place, :].astype(jnp.float32)
            sums = [total + table[c * coefs + k] * value for c, total in enumerate(sums)]
        for c in range(5):
            stress[c, place, :] = sums[c]

    @pl.loop(0, 5)
    def _(c):
        high, low = split(stress[c])
        mixed = dot(high, ahead_x[0]) + dot(high, ahead_x[1]) + dot(low, ahead_x[0])
        high, low = split(mixed)
        both = dot(ahead_y[0], high) + dot(ahead_y[0], low) + dot(ahead_y[1], high)
        cos_part, sin_part = both[:length_y], both[length_y:]
        spectrum[c, :, :slots] = cos_part[:, :slots] + sin_part[:, slots:]
        spectrum[c, :, slots:] = cos_part[:, slots:] - sin_part[:, :slots]

    filler = [jnp.zeros((message - 5 * owned, length_x), jnp.float32)] if message > 5 * owned else []

    @pl.loop(0, count)
    def _(d):
        pieces = [spectrum[c, pl.ds(d * owned, owned), :] for c in range(5)]
        send[d] = jnp.concatenate(pieces + filler, axis=0).astype(jnp.bfloat16)

    recv[me] = send[me]
    turn(send, recv, 0, lambda other: other)
    bulk(lead, lead + second)
    composite_tables(synthesis, projection, turn_projection, directions, tables)
    total_coefs = damping.shape[1]
    at_row = lax.broadcasted_iota(jnp.int32, (decay.shape[0], total_coefs), 0)
    at_lane = lax.broadcasted_iota(jnp.int32, (decay.shape[0], total_coefs), 1)
    spread = jnp.where(at_row == at_lane, damping[...] + 6.0 * transl_diff, 0.0)
    decay[...] = jnp.broadcast_to(jnp.sum(spread, axis=1, keepdims=True), decay.shape)
    arrived(recv, 0).wait()

    @pl.loop(0, spaces)
    def _(z):
        total = recv[z * groups].astype(jnp.float32)
        for g in range(1, groups):
            total = total + recv[z * groups + g].astype(jnp.float32)
        planes[z] = total

    def along_z(source, at):
        cos_part = line_z[at * spaces] * source[0]
        sin_part = line_z[spaces * spaces + at * spaces] * source[0]
        for z in range(1, spaces):
            cos_part = cos_part + line_z[at * spaces + z] * source[z]
            sin_part = sin_part + line_z[spaces * spaces + at * spaces + z] * source[z]
        return cos_part, sin_part

    kx = wave_x[...]
    ky = wave_y[pl.ds(me * owned, owned), :]

    @pl.loop(0, spaces)
    def _(m):
        cos_part, sin_part = along_z(planes, m)
        kz = line_z[2 * spaces * spaces + m]
        halves = (
            cos_part[:, :slots] + sin_part[:, slots:],
            cos_part[:, slots:] - sin_part[:, :slots],
        )
        square = kx * kx + ky * ky + kz * kz
        inverse = jnp.where(square > 0, 1.0 / jnp.where(square > 0, square, 1.0), 0.0)
        solved_halves = []
        for half in halves:
            s_xx, s_yy, s_xy, s_xz, s_yz = [half[c * owned : (c + 1) * owned] for c in range(5)]
            t_x = kx * s_xx + ky * s_xy + kz * s_xz
            t_y = kx * s_xy + ky * s_yy + kz * s_yz
            t_z = kx * s_xz + ky * s_yz
            along = (kx * t_x + ky * t_y + kz * t_z) * inverse
            solved_halves.append(
                [(t_x - kx * along) * inverse, (t_y - ky * along) * inverse, (t_z - kz * along) * inverse]
            )
        real, imag = solved_halves
        flow_real = [-w for w in imag] + [-kz * real[0], -kz * real[1]]
        flow_imag = list(real) + [-kz * imag[0], -kz * imag[1]]
        spare = [f[:, :slots] for f in filler]
        solved[m, :, :slots] = jnp.concatenate(flow_real + spare, axis=0)
        solved[m, :, slots:] = jnp.concatenate(flow_imag + spare, axis=0)

    @pl.loop(0, spaces)
    def _(z):
        cos_part, sin_part = along_z(solved, z)
        back[z, :, :slots] = (cos_part[:, :slots] - sin_part[:, slots:]).astype(jnp.bfloat16)
        back[z, :, slots:] = (cos_part[:, slots:] + sin_part[:, :slots]).astype(jnp.bfloat16)

    returned[me] = back[space_id]
    turn(back, returned, 1, lambda other: other // groups)
    bulk(lead + second, steps)
    arrived(returned, 1).wait()

    @pl.loop(0, count)
    def _(d):
        values = returned[d].astype(jnp.float32)
        for c in range(5):
            spectrum[c, pl.ds(d * owned, owned), :] = values[c * owned : (c + 1) * owned]

    def to_rows(c, with_slope):
        lines = spectrum[c].astype(jnp.bfloat16)
        used = pl.ds(0, (4 if with_slope else 2) * rows)
        both = dot(back_y[0, group_id, used, :], lines) + dot(back_y[1, group_id, used, :], lines)
        found = []
        for k in range(2 if with_slope else 1):
            cos_part, sin_part = both[2 * k * rows : (2 * k + 1) * rows], both[(2 * k + 1) * rows : (2 * k + 2) * rows]
            found.append(
                jnp.concatenate(
                    [cos_part[:, :slots] - sin_part[:, slots:], cos_part[:, slots:] + sin_part[:, :slots]],
                    axis=1,
                )
            )
        return found

    def to_cells(values, with_slope):
        high, low = split(values)
        used = slice(0, 2 * length_x if with_slope else length_x)
        return dot(high, back_x[0, :, used]) + dot(high, back_x[1, :, used]) + dot(low, back_x[0, :, used])

    gradient = [[None] * 3 for _ in range(3)]
    for i in range(3):
        plain, slope_y = to_rows(i, True)
        cells = to_cells(plain, True)
        velocity[i, 0] = cells[:, :length_x]
        flow[i] = cells[:, :length_x]
        gradient[i][0] = cells[:, length_x:]
        gradient[i][1] = to_cells(slope_y, False)
        if i < 2:
            gradient[i][2] = to_cells(to_rows(3 + i, False)[0], False)
    place = 3
    for i in range(3):
        for j in range(3):
            if i + j < 4:
                forward_term, mirror_term = gradient[i][j], gradient[j][i]
                flow[place] = 0.5 * shape_factor * (forward_term + mirror_term) + 0.5 * (
                    forward_term - mirror_term
                )
                place += 1

    @pl.loop(0, steps)
    def _(step):
        for o in range(groups - 1):
            regroup(step, o).wait()
        halo(step, 0).wait()
        halo(step, 1).wait()

    for o in range(groups - 1):
        edge(o).wait()


def stokes(coeffs, edges, table, synthesis, projection, turn_projection, damping, spaces, groups):
    coefs, _, length_y, length_x = coeffs.shape
    rows = length_y // groups
    steps = rows // chunk
    count = spaces * groups
    message = -(-5 * (length_y // count) // 16) * 16
    anywhere = pl.BlockSpec(memory_space=pl.ANY)
    vmem = pl.BlockSpec(memory_space=pltpu.VMEM)
    smem = pl.BlockSpec(memory_space=pltpu.SMEM)
    kept = coeffs.dtype
    strip = jax.ShapeDtypeStruct((coefs, rows, length_x), kept)
    padded = -(-synthesis.shape[1] // 16) * 16
    directions = jnp.asarray(sphere_directions(synthesis.shape[0]), jnp.float32)
    line_z, *others = spectral_tables(length_x, length_y, spaces, groups)
    return pl.pallas_call(
        functools.partial(stokes_kernel, spaces, groups),
        out_shape=(
            jax.ShapeDtypeStruct((groups - 1, coefs, rows, length_x), kept),
            strip,
            strip,
            jax.ShapeDtypeStruct(edges.shape, kept),
            jax.ShapeDtypeStruct((11, rows, length_x), jnp.float32),
            jax.ShapeDtypeStruct((3, 1, rows, length_x), jnp.float32),
            jax.ShapeDtypeStruct((padded, 12 * padded), kept),
            jax.ShapeDtypeStruct((padded, length_x), jnp.float32),
        ),
        in_specs=[smem, smem, anywhere] + [vmem] * 12,
        out_specs=(anywhere, anywhere, anywhere, vmem, vmem, vmem, vmem, vmem),
        scratch_shapes=[
            pltpu.VMEM((coefs, length_y, length_x), kept),
            pltpu.VMEM((5, length_y, length_x), jnp.float32),
            pltpu.VMEM((5, length_y, length_x), jnp.float32),
            pltpu.VMEM((count, message, length_x), kept),
            pltpu.VMEM((count, message, length_x), kept),
            pltpu.VMEM((spaces, message, length_x), jnp.float32),
            pltpu.VMEM((spaces, message, length_x), jnp.float32),
            pltpu.VMEM((spaces, message, length_x), kept),
            pltpu.VMEM((count, message, length_x), kept),
            pltpu.SemaphoreType.DMA((length_y // chunk,)),
            pltpu.SemaphoreType.DMA((groups - 1, steps)),
            pltpu.SemaphoreType.DMA((groups - 1, steps)),
            pltpu.SemaphoreType.DMA((2, steps)),
            pltpu.SemaphoreType.DMA((2, steps)),
            pltpu.SemaphoreType.DMA((groups - 1,)),
            pltpu.SemaphoreType.DMA((groups - 1,)),
            pltpu.SemaphoreType.DMA((2, 2)),
        ],
        compiler_params=pltpu.CompilerParams(
            collective_id=0, has_side_effects=True, vmem_limit_bytes=VMEM_BYTES
        ),
    )(
        table,
        line_z,
        coeffs,
        edges,
        *others,
        synthesis,
        projection,
        turn_projection,
        damping.reshape(1, -1),
        directions,
    )


def rate_kernel(
    spaces,
    groups,
    coeffs,
    mid,
    below,
    above,
    edges,
    flow,
    tables,
    decay,
    shifts,
    rate,
    lines,
    mid_part,
    below_part,
    above_part,
    below_far,
    above_far,
    flat,
    slope_x,
    smooth,
    even,
    odd,
    stage,
    far_send,
    far_recv,
    load_sem,
    out_send,
    out_recv,
    own_sem,
):
    space_id, group_id, lower, upper, others = ring_partners(spaces, groups)
    coefs, _, _, length_x = coeffs.shape
    rows = mid.shape[2]
    steps = rows // chunk
    total = groups * coefs
    padded = lines.shape[1]
    greet([lower, upper] + others)

    def part(step):
        return pl.ds(pl.multiple_of(step * chunk, chunk), chunk)

    def far(step, side):
        return pltpu.make_async_remote_copy(
            src_ref=mid.at[:, :, part(step)],
            dst_ref=(above_far if side == 0 else below_far).at[:, :, part(step)],
            send_sem=far_send.at[side, step],
            recv_sem=far_recv.at[side, step],
            device_id=lower if side == 0 else upper,
            device_id_type=MESH,
        )

    own_rows = group_id * rows

    def mid_loads(step):
        slot = lax.rem(step, 2)
        own = pltpu.make_async_copy(
            coeffs.at[:, 0, pl.ds(pl.multiple_of(own_rows + step * chunk, chunk), chunk)],
            mid_part.at[slot, pl.ds(group_id * coefs, coefs)],
            load_sem.at[slot, 0],
        )
        rest = [
            pltpu.make_async_copy(
                mid.at[o, :, part(step)],
                mid_part.at[slot, pl.ds(others[o][1] * coefs, coefs)],
                load_sem.at[slot, 3 + o],
            )
            for o in range(groups - 1)
        ]
        return [own] + rest

    def halo_loads(step):
        slot = lax.rem(step, 2)
        return [
            pltpu.make_async_copy(below.at[:, part(step)], below_part.at[slot], load_sem.at[slot, 1]),
            pltpu.make_async_copy(above.at[:, part(step)], above_part.at[slot], load_sem.at[slot, 2]),
        ]

    @pl.loop(0, min(ahead, steps))
    def _(step):
        far(step, 0).start()
        far(step, 1).start()

    for copy in mid_loads(0) + halo_loads(0):
        copy.start()

    lanes = 128
    halves_x = length_x // lanes
    zeros = jnp.zeros((padded - total, length_x), jnp.float32)
    for side, line in ((0, 0), (1, rows + 1)):
        pieces = [edges[g, side].astype(jnp.float32) for g in range(groups)]
        lines[line] = jnp.concatenate(pieces + ([zeros] if padded > total else []), axis=0).astype(jnp.bfloat16)

    def columns(row):
        values = jnp.concatenate(
            [flat[half, pl.ds(row, total, stride=chunk), :] for half in range(halves_x)], axis=1
        )
        return jnp.concatenate([values, zeros], axis=0) if padded > total else values

    def transpose_mid(step):
        for copy in mid_loads(step):
            copy.wait()
        slot = lax.rem(step, 2)
        for half in range(halves_x):
            cut = slice(half * lanes, (half + 1) * lanes)
            flat[half] = mid_part[slot, :, :, cut].astype(jnp.float32).reshape(total * chunk, lanes)
        for row in range(chunk):
            lines[step * chunk + 1 + row] = columns(row).astype(jnp.bfloat16)

    def out_copies(step):
        slot = lax.rem(step, 2)
        place = pl.ds(pl.multiple_of(own_rows + step * chunk, chunk), chunk)
        own = pltpu.make_async_copy(
            stage.at[slot, pl.ds(group_id * coefs, coefs)], rate.at[:, 0, place], own_sem.at[slot]
        )
        rest = [
            pltpu.make_async_remote_copy(
                src_ref=stage.at[slot, pl.ds(others[o][1] * coefs, coefs)],
                dst_ref=rate.at[:, 0, place],
                send_sem=out_send.at[o, step],
                recv_sem=out_recv.at[groups - 2 - o, step],
                device_id=others[o],
                device_id_type=MESH,
            )
            for o in range(groups - 1)
        ]
        return own, rest

    transpose_mid(0)

    @pl.loop(0, steps)
    def _(step):
        slot = lax.rem(step, 2)

        @pl.when(step + ahead < steps)
        def _():
            far(step + ahead, 0).start()
            far(step + ahead, 1).start()

        @pl.when(step + 1 < steps)
        def _():
            for copy in mid_loads(step + 1) + halo_loads(step + 1):
                copy.start()

        start = pl.multiple_of(step * chunk, chunk)
        block = lines[pl.ds(start + 1, chunk)].reshape(chunk * padded, length_x)
        slope_x[...] = jnp.dot(block, shifts[0], preferred_element_type=jnp.float32).astype(jnp.bfloat16)
        smooth[...] = jnp.dot(block, shifts[1], preferred_element_type=jnp.float32)

        @pl.when(step + 1 < steps)
        def _():
            transpose_mid(step + 1)

        for copy in halo_loads(step):
            copy.wait()
        far(step, 0).wait_recv()
        far(step, 1).wait_recv()

        def halves(o):
            if o < 0:
                return group_id, below_part[slot].astype(jnp.float32), above_part[slot].astype(jnp.float32)
            return (
                others[o][1],
                below_far[o, :, part(step)].astype(jnp.float32),
                above_far[o, :, part(step)].astype(jnp.float32),
            )

        size = coefs * chunk
        for o in range(-1, groups - 1):
            group, low, high = halves(o)
            for half in range(halves_x):
                cut = slice(half * lanes, (half + 1) * lanes)
                slope = 0.5 * (high[:, :, cut] - low[:, :, cut])
                flat[half, pl.ds(pl.multiple_of(group * size, 8), size), :] = slope.reshape(size, lanes)

        inputs = (even, odd)

        def prepare(row, slot):
            line = start + 1 + row
            center = lines[line]
            high_y = lines[line + 1].astype(jnp.float32)
            low_y = lines[line - 1].astype(jnp.float32)
            slope_z = columns(row)
            slope_y = 0.5 * (high_y - low_y)
            first = slope_x[pl.ds(pl.multiple_of(row * padded, padded), padded), :]
            here = start + row

            def field(i):
                return flow[i, pl.ds(here, 1), :]

            inputs[slot][0:padded] = first
            inputs[slot][padded : 2 * padded] = slope_y.astype(jnp.bfloat16)
            inputs[slot][2 * padded : 3 * padded] = slope_z.astype(jnp.bfloat16)
            carried = field(0) * first.astype(jnp.float32) + field(1) * slope_y + field(2) * slope_z
            inputs[slot][3 * padded : 4 * padded] = carried.astype(jnp.bfloat16)
            for i in range(8):
                inputs[slot][(4 + i) * padded : (5 + i) * padded] = center * field(3 + i).astype(jnp.bfloat16)

        def finish(row, slot):
            line = start + 1 + row
            at = pl.ds(pl.multiple_of(row * padded, padded), padded)
            result = jnp.dot(tables[...], inputs[slot][...], preferred_element_type=jnp.float32)
            around = lines[line + 1].astype(jnp.float32) + lines[line - 1].astype(jnp.float32)
            result = result + smooth[at, :] + transl_diff * around
            smooth[at, :] = result - decay[...] * lines[line].astype(jnp.float32)

        prepare(0, 0)

        @pl.loop(0, chunk // 2 - 1)
        def _(pair):
            prepare(2 * pair + 1, 1)
            finish(2 * pair, 0)
            prepare(2 * pair + 2, 0)
            finish(2 * pair + 1, 1)

        prepare(chunk - 1, 1)
        finish(chunk - 2, 0)
        finish(chunk - 1, 1)

        for row in range(chunk):
            for half in range(halves_x):
                cut = slice(half * lanes, (half + 1) * lanes)
                flat[half, pl.ds(row, total, stride=chunk), :] = smooth[pl.ds(row * padded, total), cut]

        @pl.when(step >= 2)
        def _():
            own, rest = out_copies(step - 2)
            own.wait()
            for copy in rest:
                copy.wait_send()

        for o in range(-1, groups - 1):
            group, low, high = halves(o)
            for half in range(halves_x):
                cut = slice(half * lanes, (half + 1) * lanes)
                value = flat[half, pl.ds(pl.multiple_of(group * size, 8), size), :].reshape(coefs, chunk, lanes)
                value = value + transl_diff * (high[:, :, cut] + low[:, :, cut])
                stage[slot, pl.ds(group * coefs, coefs), :, cut] = value.astype(jnp.bfloat16)
        own, rest = out_copies(step)
        own.start()
        for copy in rest:
            copy.start()

    for step in range(max(steps - 2, 0), steps):
        own, rest = out_copies(step)
        own.wait()
        for copy in rest:
            copy.wait_send()

    @pl.loop(0, steps)
    def _(step):
        far(step, 0).wait_send()
        far(step, 1).wait_send()
        for copy in out_copies(step)[1]:
            copy.wait_recv()


def rates(coeffs, mid, below, above, edges, flow, tables, decay, shifts, spaces, groups):
    coefs, _, length_y, length_x = coeffs.shape
    rows = length_y // groups
    steps = rows // chunk
    total = groups * coefs
    padded = tables.shape[0]
    anywhere = pl.BlockSpec(memory_space=pl.ANY)
    vmem = pl.BlockSpec(memory_space=pltpu.VMEM)
    kept = coeffs.dtype
    return pl.pallas_call(
        functools.partial(rate_kernel, spaces, groups),
        out_shape=jax.ShapeDtypeStruct(coeffs.shape, kept),
        in_specs=[anywhere] * 4 + [vmem] * 5,
        out_specs=anywhere,
        scratch_shapes=[
            pltpu.VMEM((rows + 2, padded, length_x), kept),
            pltpu.VMEM((2, total, chunk, length_x), kept),
            pltpu.VMEM((2, coefs, chunk, length_x), kept),
            pltpu.VMEM((2, coefs, chunk, length_x), kept),
            pltpu.VMEM((groups - 1, coefs, rows, length_x), kept),
            pltpu.VMEM((groups - 1, coefs, rows, length_x), kept),
            pltpu.VMEM((length_x // 128, total * chunk, 128), jnp.float32),
            pltpu.VMEM((chunk * padded, length_x), kept),
            pltpu.VMEM((chunk * padded, length_x), jnp.float32),
            pltpu.VMEM((tables.shape[1], length_x), kept),
            pltpu.VMEM((tables.shape[1], length_x), kept),
            pltpu.VMEM((2, total, chunk, length_x), kept),
            pltpu.SemaphoreType.DMA((2, steps)),
            pltpu.SemaphoreType.DMA((2, steps)),
            pltpu.SemaphoreType.DMA((2, groups + 2)),
            pltpu.SemaphoreType.DMA((groups - 1, steps)),
            pltpu.SemaphoreType.DMA((groups - 1, steps)),
            pltpu.SemaphoreType.DMA((2,)),
        ],
        compiler_params=pltpu.CompilerParams(
            collective_id=1, has_side_effects=True, vmem_limit_bytes=VMEM_BYTES
        ),
    )(coeffs, mid, below, above, edges, flow, tables, decay, shifts)


def shift_tables(length):
    eye = np.eye(length)
    after, before = np.roll(eye, 1, 0), np.roll(eye, -1, 0)
    return jnp.asarray(np.stack([0.5 * (after - before), transl_diff * (after + before)]).astype(jnp.bfloat16))


def boundary_rows(coeffs, groups):
    rows = coeffs.shape[2] // groups
    found = []
    for group in range(groups):
        for row in ((group * rows - 1) % (groups * rows), (group + 1) * rows % (groups * rows)):
            found.append(coeffs[:, 0, row])
    return jnp.stack(found).reshape(groups, 2, coeffs.shape[0], coeffs.shape[3])


def local(coeffs, synthesis, projection, turn_projection, damping):
    spaces = lax.axis_size("space")
    groups = lax.axis_size("harm")
    group_id = lax.axis_index("harm")
    local_coefs, _, _, length_x = coeffs.shape
    table = moment_table(synthesis)
    own_table = lax.dynamic_slice_in_dim(table, group_id * local_coefs, local_coefs, 1)
    own_table = own_table.astype(jnp.float32)
    own_table = jnp.stack(
        [own_table[0] - own_table[2], own_table[1] - own_table[2], own_table[3], own_table[4], own_table[5]]
    )
    mid, below, above, edges, flow, velocity, tables, decay = stokes(
        coeffs,
        boundary_rows(coeffs, groups),
        own_table.reshape(-1),
        synthesis,
        projection,
        turn_projection,
        damping,
        spaces,
        groups,
    )
    rate = rates(
        coeffs, mid, below, above, edges, flow, tables, decay, shift_tables(length_x), spaces, groups
    )
    return (rate, velocity)


def solution(mesh):
    in_specs = (P("harm", "space", None, None), P(), P(), P(), P())
    out_specs = (P("harm", "space", None, None), P(None, "space", "harm", None))
    return jax.shard_map(local, mesh=mesh, in_specs=in_specs, out_specs=out_specs, check_vma=False)
```
